32 devices in a mesh: groups: 2 (over y), tm: 4 (over z), stn: 4 (over x, core).
Axes of the slice: x: 2, y: 2, z: 4, core: 2. Of those that a mesh axis runs over, the one named last changes fastest.
Arguments:
- right_side: float32 [256, 7168], P(('groups', 'tm'), 'stn'), parts along dimension 0, may hold values from -8 to 8
- mask: int32 [16, 7168], P(('groups', 'tm'), 'stn'), parts along dimension 0, may hold values 0 or 1
- coords: int32 [2, 14336], P(None, ('groups', 'stn')), parts along dimension 1, may hold values from 0 to 255
- station_scale: float32 [14336], P(('groups', 'stn')), parts along dimension 0, may hold values from 0.5 to 2
Outputs:
- solution_field: float32 [256, 7168], P(('groups', 'tm'), 'stn'), parts along dimension 0
- residual: float32 [256, 7168], P(('groups', 'tm'), 'stn'), parts along dimension 0
The draws below stay inside these ranges and needn't reach their ends.
There are 2 independent parts, one for each index of `groups`. The reference program is written for one: setup_inputs(seed, part) draws one part's arguments, and reference() takes and returns one part's arrays. A program takes and returns all parts, laid end to end along the dimension named above; each array names one. Nothing has to cross between parts.
All inputs are finite; a program needn't handle non-finite values. No bound on the sum of `mask` on one device may be relied on, other than what follows from the above.
Results may differ from the reference program's by a relative error of at most 0.015.
Values may be sent and summed in bfloat16 or wider, within the bound.
No kernel may reach another device: no remote copies, remote signals or barrier semaphores. Data moves between devices by JAX's collectives and lax.ppermute only.
A program may use at most 64 MiB of HBM per device.

```python
import math
import jax
import jax.numpy as jnp
from jax import lax

S = 7168
H_DEV = 32
MB = 16
GRID = 256
ITERS = 2
H = 128
NBLK = 8


def draw_right_side(key, part):
    first = jax.random.fold_in(key, 11)
    second = jax.random.fold_in(key, 12)
    hours = jnp.arange(H, dtype=jnp.float32)
    ramp = 0.6 + 1.2 * hours / (H - 1.0)
    station_factor = jnp.exp(jax.random.uniform(second, (S,), jnp.float32, -0.35, 0.35))
    noise = jax.random.normal(first, (H, S), jnp.float32)
    values = noise * ramp[:, None] * station_factor[None, :]
    return jnp.clip(values, -8.0, 8.0)


def place_ends(drawn, rng, low, top_value):
    longest = drawn.shape.index(max(drawn.shape))
    spots = []
    for shift in (0, 1):
        where = [jax.random.randint(jax.random.fold_in(rng, axis), (), 0, length) for axis, length in enumerate(drawn.shape)]
        where[longest] = (where[longest] + shift) % drawn.shape[longest]
        spots.append(tuple(where))
    return drawn.at[spots[0]].set(low).at[spots[1]].set(top_value)


def level_of(key, extent, cuts, low, largest):
    gain, own = 1.0, jax.random.fold_in(key, 6)
    for position, shards_of in cuts:
        heights = jnp.exp(jax.random.uniform(jax.random.fold_in(own, position), (shards_of,), jnp.float32, low / len(cuts), largest / len(cuts)))
        gain = gain * jnp.repeat(heights, extent[position] // shards_of).reshape([-1 if axis == position else 1 for axis in range(len(extent))])
    return gain


def setup_inputs(seed: int = 0, part: int = 0) -> dict:
    arg_keys = jax.random.split(jax.random.key(seed), 5)
    part_keys = jax.random.split(jax.random.fold_in(arg_keys[4], part), 5)
    return {
        "right_side": draw_right_side(jax.random.fold_in(jax.random.fold_in(arg_keys[4], part), 71), part),
        "mask": place_ends((jax.random.randint(part_keys[1], (NBLK, S), 0, 4) < 3).astype(jnp.int32), jax.random.fold_in(part_keys[1], 1), 0, 1),
        "coords": place_ends(jax.random.randint(part_keys[2], (2, S), 0, GRID), jax.random.fold_in(part_keys[2], 1), 0, GRID - 1).astype(jnp.int32),
        "station_scale": jnp.clip(jnp.exp(math.log(2.0) - 1.3862944 * jax.random.uniform(part_keys[3], (S,), jnp.float32) ** level_of(part_keys[3], (S,), ((0, 4),), -0.2, 0.2)), 0.5, 2.0),
    }


root_three = 1.7320508075688772
kernel_norm = 4.0
noise_level = 0.5

def matern(rows, cols):
    rowf = rows.astype(jnp.float32)
    colf = cols.astype(jnp.float32)
    delta_x = rowf[0][:, None] - colf[0][None, :]
    delta_y = rowf[1][:, None] - colf[1][None, :]
    scaled = root_three * jnp.sqrt(delta_x * delta_x + delta_y * delta_y) * 4.0 / GRID
    return ((1.0 + scaled) * jnp.exp(-scaled) / kernel_norm).astype(jnp.bfloat16)

def lag_weight(lag):
    frac = jnp.abs(lag) / (H_DEV + 1.0)
    inner = jnp.maximum(1.0 - frac, 0.0)
    weight = inner ** 4 * (4.0 * frac + 1.0) / H_DEV
    return jnp.where(jnp.abs(lag) <= H_DEV, weight, 0.0)

def time_apply(spread):
    padded = jnp.pad(spread, ((H_DEV, H_DEV), (0, 0)))
    hours = spread.shape[0]

    def step(index, total):
        lag = (index - H_DEV).astype(jnp.float32)
        start = (2 * H_DEV - index).astype(jnp.int32)
        piece = lax.dynamic_slice_in_dim(padded, start, hours, 0)
        return total + lag_weight(lag) * piece
    return lax.fori_loop(jnp.int32(0), jnp.int32(2 * H_DEV + 1), step, jnp.zeros(spread.shape, jnp.float32))

def reference(right_side, mask, coords, station_scale):
    observed = jnp.repeat(mask, MB, axis=0).astype(jnp.float32)
    kernel = matern(coords, coords).astype(jnp.float32)

    def operate(field):
        masked = (observed * station_scale[None, :] * field).astype(jnp.bfloat16)
        spread = jnp.dot(masked.astype(jnp.float32), kernel, precision=lax.Precision.HIGHEST)
        spread = station_scale[None, :] * spread
        return observed * time_apply(spread) + noise_level * field
    solution_field = jnp.zeros_like(right_side)
    residual, direction = (right_side, right_side)
    norm_now = jnp.sum(residual * residual)
    for step in range(ITERS):
        image = operate(direction)
        alpha = norm_now / jnp.sum(direction * image)
        solution_field = solution_field + alpha * direction
        residual = residual - alpha * image
        norm_next = jnp.sum(residual * residual)
        direction = residual + norm_next / norm_now * direction
        norm_now = norm_next
    return (solution_field, residual)
```

```python
import jax
import jax.numpy as jnp
from jax import lax
from jax.sharding import PartitionSpec as P

MB = 16
GRID = 256
ITERS = 2


root_three = 1.7320508075688772
kernel_norm = 4.0
noise_level = 0.5


def with_halo(block, sides, width):
    for axis, dim in sides:
        count = lax.axis_size(axis)
        forward = [(i, i + 1) for i in range(count - 1)]
        backward = [(target, source) for source, target in forward]
        low = lax.ppermute(
            lax.slice_in_dim(block, block.shape[dim] - width, None, axis=dim), axis, forward
        )
        high = lax.ppermute(lax.slice_in_dim(block, 0, width, axis=dim), axis, backward)
        block = jnp.concatenate([low, block, high], axis=dim)
    return block


def matern(rows, cols):
    rowf = rows.astype(jnp.float32)
    colf = cols.astype(jnp.float32)
    delta_x = rowf[0][:, None] - colf[0][None, :]
    delta_y = rowf[1][:, None] - colf[1][None, :]
    scaled = root_three * jnp.sqrt(delta_x * delta_x + delta_y * delta_y) * 4.0 / GRID
    return ((1.0 + scaled) * jnp.exp(-scaled) / kernel_norm).astype(jnp.bfloat16)


def band_matrix(hours_dev):
    rows = lax.broadcasted_iota(jnp.int32, (hours_dev, 3 * hours_dev), 0)
    cols = lax.broadcasted_iota(jnp.int32, (hours_dev, 3 * hours_dev), 1)
    lag = (rows + hours_dev - cols).astype(jnp.float32)
    frac = jnp.abs(lag) / (hours_dev + 1.0)
    inner = jnp.maximum(1.0 - frac, 0.0)
    weight = inner**4 * (4.0 * frac + 1.0) / hours_dev
    return jnp.where(jnp.abs(lag) <= hours_dev, weight, 0.0)


def station_panels(masked, my_coords):
    tile = matern(lax.all_gather(my_coords, "stn", axis=1, tiled=True), my_coords)
    return jnp.dot(
        lax.all_gather(masked, "stn", axis=1, tiled=True), tile, preferred_element_type=jnp.float32
    )


def two_sums(residual, image):
    axes = ("tm", "stn")
    count = lax.axis_size(axes)
    parts = jnp.stack([jnp.sum(residual * residual), jnp.sum(residual * image)])
    rows = jnp.broadcast_to(parts[None, :, None], (count, 2, 128))
    rows = lax.all_to_all(rows, axes, 0, 0, tiled=True)
    sums = jnp.sum(rows, axis=0)
    return sums[0, 0], sums[1, 0]


def local(right_side, mask, coords, station_scale):
    hours_dev = right_side.shape[0]
    observed = jnp.repeat(mask, MB, axis=0).astype(jnp.float32)
    my_coords = coords.astype(jnp.bfloat16)
    band = band_matrix(hours_dev)
    scale_row = station_scale[None, :]

    def operate(field):
        masked = (observed * scale_row * field).astype(jnp.bfloat16)
        spread = station_panels(masked, my_coords)
        spread = scale_row * spread
        padded = with_halo(spread.astype(jnp.bfloat16), (("tm", 0),), hours_dev).astype(
            spread.dtype
        )
        smoothed = jnp.dot(
            band, padded, precision=lax.Precision.HIGHEST, preferred_element_type=jnp.float32
        )
        return observed * smoothed + noise_level * field

    solution_field = jnp.zeros_like(right_side)
    residual = right_side
    image = operate(residual)
    norm_now, product = two_sums(residual, image)
    alpha = norm_now / product
    direction, along = (residual, image)
    for step in range(ITERS):
        solution_field = solution_field + alpha * direction
        residual = residual - alpha * along
        if step + 1 < ITERS:
            image = operate(residual)
            norm_next, product = two_sums(residual, image)
            ratio = norm_next / norm_now
            alpha = norm_next / (product - ratio * norm_next / alpha)
            direction = residual + ratio * direction
            along = image + ratio * along
            norm_now = norm_next
    return (solution_field, residual)


def solution(mesh):
    placed = (
        P(("groups", "tm"), "stn"),
        P(("groups", "tm"), "stn"),
        P(None, ("groups", "stn")),
        P(("groups", "stn")),
    )
    return jax.shard_map(
        local,
        mesh=mesh,
        in_specs=placed,
        out_specs=(P(("groups", "tm"), "stn"), P(("groups", "tm"), "stn")),
        check_vma=False,
    )
```

```python
import functools
import math

import jax
import jax.numpy as jnp
from jax import lax
from jax.experimental import pallas as pl
from jax.experimental.pallas import tpu as pltpu
from jax.sharding import PartitionSpec as P


GRID = 256
kernel_norm = 4.0
noise_level = 0.5
slope = math.sqrt(3.0) * 4.0 / GRID
LANES = 128
VMEM = pl.BlockSpec(memory_space=pltpu.VMEM)
MIB = 1024 * 1024


def call(body, out_shape, args, scratch=(), limit=16):
    outs = jax.tree.map(lambda _: VMEM, out_shape)
    return pl.pallas_call(
        body,
        out_shape=out_shape,
        in_specs=[VMEM] * len(args),
        out_specs=outs,
        scratch_shapes=list(scratch),
        compiler_params=pltpu.CompilerParams(vmem_limit_bytes=limit * MIB),
    )(*args)


def features(coords, rows):
    centred = coords.astype(jnp.float32) - GRID / 2.0
    x, y = centred[0:1], centred[1:2]
    square = x * x + y * y
    high = jnp.floor(square * (1.0 / 256.0)) * 256.0
    low = square - high
    one, zero = jnp.ones_like(x), jnp.zeros_like(x)
    if rows:
        return jnp.concatenate([x, y, high, low, one, one, zero, zero], axis=0)
    return jnp.concatenate([-2.0 * x, -2.0 * y, one, one, high, low, zero, zero], axis=0)


def step_of(extent):
    for step in (448, 256, 128, 64, 32, 16):
        if extent % step == 0:
            return step
    return extent


def tile_body(rows_ref, cols_ref, tile_ref, row_features, col_features):
    row_features[...] = features(rows_ref[...], True).T.astype(jnp.bfloat16)
    col_features[...] = features(cols_ref[...], False).astype(jnp.bfloat16)
    step = step_of(tile_ref.shape[0])

    def body(index, carry):
        at = pl.ds(pl.multiple_of(index * step, step), step)
        square = jnp.dot(
            row_features[at, :], col_features[...], preferred_element_type=jnp.float32
        )
        distance = square * lax.rsqrt(jnp.maximum(square, 1e-20))
        decay = jnp.exp2(distance * (-slope * math.log2(math.e)))
        tile_ref[at, :] = ((1.0 / kernel_norm + slope / kernel_norm * distance) * decay).astype(
            jnp.bfloat16
        )
        return carry

    lax.fori_loop(0, tile_ref.shape[0] // step, body, 0)


def matern_tile(rows, cols):
    extent, width = rows.shape[1], cols.shape[1]
    return call(
        tile_body,
        jax.ShapeDtypeStruct((extent, width), jnp.bfloat16),
        (rows, cols),
        scratch=[pltpu.VMEM((extent, 8), jnp.bfloat16), pltpu.VMEM((8, width), jnp.bfloat16)],
    )


def observed_rows(mask_ref, hours):
    block = hours // mask_ref.shape[0]
    width = mask_ref.shape[1]
    mask = mask_ref[...].astype(jnp.float32)
    return jnp.concatenate(
        [jnp.broadcast_to(mask[b : b + 1], (block, width)) for b in range(mask_ref.shape[0])],
        axis=0,
    )


def mask_body(field_ref, mask_ref, scale_ref, out_ref):
    gain = observed_rows(mask_ref, field_ref.shape[0]) * scale_ref[...]
    out_ref[...] = (gain * field_ref[...]).astype(out_ref.dtype)


def smooth_body(low_ref, own_ref, high_ref, out_ref):
    hours = own_ref.shape[0]
    rows = lax.broadcasted_iota(jnp.int32, (hours, 3 * hours), 0)
    cols = lax.broadcasted_iota(jnp.int32, (hours, 3 * hours), 1)
    lag = jnp.abs((rows + hours - cols).astype(jnp.float32))
    frac = lag / (hours + 1.0)
    inner = jnp.maximum(1.0 - frac, 0.0)
    squared = inner * inner
    weight = squared * squared * (4.0 * frac + 1.0) / hours
    weight = jnp.where(lag <= hours, weight, 0.0)
    top = weight.astype(jnp.bfloat16)
    rest = (weight - top.astype(jnp.float32)).astype(jnp.bfloat16)
    field = jnp.concatenate([low_ref[...], own_ref[...], high_ref[...]], axis=0)
    both = jnp.dot(
        jnp.concatenate([top, rest], axis=0), field, preferred_element_type=jnp.float32
    )
    out_ref[...] = (both[:hours] + both[hours:]).astype(out_ref.dtype)


def smoothed(field):
    count = lax.axis_size("tm")
    up = [(i, i + 1) for i in range(count - 1)]
    down = [(i + 1, i) for i in range(count - 1)]
    low = lax.ppermute(field, "tm", up)
    high = lax.ppermute(field, "tm", down)
    return call(smooth_body, jax.ShapeDtypeStruct(field.shape, field.dtype), (low, field, high))


def spread_of(blocks, tiles):
    total = jnp.dot(blocks[0], tiles[0][...], preferred_element_type=jnp.float32)
    for block, tile in zip(blocks[1:], tiles[1:]):
        total += jnp.dot(block, tile[...], preferred_element_type=jnp.float32)
    return total


def first_body(count, *refs):
    blocks, tiles = refs[:count], refs[count : 2 * count]
    field_ref, mask_ref, scale_ref, image_ref, masked_ref = refs[2 * count :]
    spread = spread_of([block[...] for block in blocks], tiles)
    gain = observed_rows(mask_ref, field_ref.shape[0]) * scale_ref[...]
    image = gain * spread + noise_level * field_ref[...]
    image_ref[...] = image
    masked_ref[...] = (gain * image).astype(masked_ref.dtype)


def total(value):
    return jnp.sum(jnp.sum(value, axis=0, keepdims=True), axis=1, keepdims=True)


def second_body(count, gathered_ref, *refs):
    me = lax.axis_index("stn")
    tiles = refs[:count]
    field_ref, image_ref, mask_ref, scale_ref, second_ref, sums_ref = refs[count:]
    spread = spread_of([gathered_ref[lax.rem(me + k, count)] for k in range(count)], tiles)
    gain = observed_rows(mask_ref, field_ref.shape[0]) * scale_ref[...]
    field, image = field_ref[...], image_ref[...]
    second = gain * spread + noise_level * image
    second_ref[...] = second
    norm, product = total(field * field), total(field * image)
    guess = norm / jnp.maximum(jnp.maximum(product, noise_level * norm), 1e-30)
    near = field - guess * image
    near_image = image - guess * second
    values = (
        norm,
        product,
        guess,
        total(near * near),
        total(near * image),
        total(image * image),
        total(near * near_image),
        total(near * second + image * near_image),
        total(image * second),
    )
    lane = lax.broadcasted_iota(jnp.int32, sums_ref.shape, 1)
    row = jnp.zeros(sums_ref.shape, jnp.float32)
    for index, value in enumerate(values):
        row = jnp.where(lane == index, value, row)
    sums_ref[...] = row


def last_body(sums_ref, field_ref, image_ref, second_ref, solution_ref, residual_ref):
    sums = sums_ref[...]
    norm, product, guess, near2, near_image, image2, cross0, cross1, cross2 = (
        sums[:, k : k + 1] for k in range(9)
    )
    norm_now, product_now = total(norm), total(product)
    alpha = norm_now / product_now
    off = alpha - guess
    norm_next = total(near2 - 2.0 * off * near_image + off * off * image2)
    product_next = total(cross0 - off * cross1 + off * off * cross2)
    ratio = norm_next / norm_now
    alpha_next = norm_next / (product_next - ratio * norm_next / alpha)
    field, image = field_ref[...], image_ref[...]
    residual = field - alpha * image
    along = (image - alpha * second_ref[...]) + ratio * image
    direction = residual + ratio * field
    solution_ref[...] = alpha * field + alpha_next * direction
    residual_ref[...] = residual - alpha_next * along


def local(right_side, mask, coords, station_scale):
    count = lax.axis_size("stn")
    everyone = count * lax.axis_size("tm")
    hours, width = right_side.shape
    scale = station_scale[None, :]
    block = jax.ShapeDtypeStruct((hours, width), jnp.bfloat16)
    wide = jax.ShapeDtypeStruct((hours, width), jnp.float32)

    def from_ahead(value, offset):
        if offset == 0:
            return value
        return lax.ppermute(value, "stn", [((i + offset) % count, i) for i in range(count)])

    masked = call(mask_body, block, (right_side, mask, scale))
    tiles = []
    for k in range(count):
        rows = from_ahead(coords, k)
        tiles.append(matern_tile(rows, coords))
    smooth = smoothed(masked)
    blocks = [from_ahead(smooth, k) for k in range(count)]
    image, masked = call(
        functools.partial(first_body, count),
        (wide, block),
        (*blocks, *tiles, right_side, mask, scale),
    )
    gathered = lax.all_gather(smoothed(masked), "stn")
    second, sums = call(
        functools.partial(second_body, count),
        (wide, jax.ShapeDtypeStruct((everyone, LANES), jnp.float32)),
        (gathered, *tiles, right_side, image, mask, scale),
    )
    sums = lax.all_to_all(sums, ("tm", "stn"), 0, 0, tiled=True)
    return call(last_body, (wide, wide), (sums, right_side, image, second))


def solution(mesh):
    placed = (
        P(("groups", "tm"), "stn"),
        P(("groups", "tm"), "stn"),
        P(None, ("groups", "stn")),
        P(("groups", "stn")),
    )
    return jax.shard_map(
        local,
        mesh=mesh,
        in_specs=placed,
        out_specs=(P(("groups", "tm"), "stn"), P(("groups", "tm"), "stn")),
        check_vma=False,
    )
```

```python
import functools
import math

import jax
import jax.numpy as jnp
from jax import lax
from jax.experimental import pallas as pl
from jax.experimental.pallas import tpu as pltpu
from jax.sharding import PartitionSpec as P


GRID = 256
kernel_norm = 4.0
noise_level = 0.5
slope = math.sqrt(3.0) * 4.0 / GRID
LANES = 128
MIB = 1024 * 1024
VMEM = pl.BlockSpec(memory_space=pltpu.VMEM)
HBM = pl.BlockSpec(memory_space=pltpu.HBM)


def call(body, out_shape, args, in_specs=None, scratch=()):
    return pl.pallas_call(
        body,
        out_shape=out_shape,
        in_specs=in_specs or [VMEM] * len(args),
        out_specs=jax.tree.map(lambda _: VMEM, out_shape),
        scratch_shapes=list(scratch),
        compiler_params=pltpu.CompilerParams(vmem_limit_bytes=16 * MIB),
    )(*args)


def load_body(field_hbm, mask_hbm, coords_hbm, scale_hbm, field, coords, gain, masked, mask, scale, sems):
    pairs = ((mask_hbm, mask), (scale_hbm, scale), (field_hbm, field), (coords_hbm, coords))
    copies = [
        pltpu.make_async_copy(source, target, sems.at[k])
        for k, (source, target) in enumerate(pairs)
    ]
    for copy in copies:
        copy.start()
    for copy in copies:
        copy.wait()
    hours, width = field.shape
    block = hours // mask.shape[0]
    observed = mask[...].astype(jnp.float32)
    observed = jnp.concatenate(
        [jnp.broadcast_to(observed[b : b + 1], (block, width)) for b in range(mask.shape[0])],
        axis=0,
    )
    gain[...] = observed * scale[...]
    masked[...] = (gain[...] * field[...]).astype(masked.dtype)


def load(right_side, mask, coords, scale):
    return call(
        load_body,
        (
            jax.ShapeDtypeStruct(right_side.shape, right_side.dtype),
            jax.ShapeDtypeStruct(coords.shape, coords.dtype),
            jax.ShapeDtypeStruct(right_side.shape, jnp.float32),
            jax.ShapeDtypeStruct(right_side.shape, jnp.bfloat16),
        ),
        (right_side, mask, coords, scale),
        in_specs=[HBM] * 4,
        scratch=[
            pltpu.VMEM(mask.shape, mask.dtype),
            pltpu.VMEM(scale.shape, scale.dtype),
            pltpu.SemaphoreType.DMA((4,)),
        ],
    )


def features(coords, rows):
    centred = coords.astype(jnp.float32) - GRID / 2.0
    x, y = centred[0:1], centred[1:2]
    square = x * x + y * y
    high = jnp.floor(square * (1.0 / 256.0)) * 256.0
    low = square - high
    one, zero = jnp.ones_like(x), jnp.zeros_like(x)
    if rows:
        return jnp.concatenate([x, y, high, low, one, one, zero, zero], axis=0)
    return jnp.concatenate([-2.0 * x, -2.0 * y, one, one, high, low, zero, zero], axis=0)


def step_of(extent):
    for step in (896, 512, 256, 128, 64, 32, 16):
        if extent % step == 0:
            return step
    return extent


def tile_body(rows_ref, cols_ref, tile_ref, row_features, col_features):
    row_features[...] = features(rows_ref[...], True).T.astype(jnp.bfloat16)
    col_features[...] = features(cols_ref[...], False).astype(jnp.bfloat16)
    step = step_of(tile_ref.shape[0])

    def body(index, carry):
        at = pl.ds(pl.multiple_of(index * step, step), step)
        square = jnp.dot(
            row_features[at, :], col_features[...], preferred_element_type=jnp.float32
        )
        distance = square * lax.rsqrt(jnp.maximum(square, 1e-20))
        decay = jnp.exp2(distance * (-slope * math.log2(math.e)))
        tile_ref[at, :] = ((1.0 / slope + distance) * decay).astype(jnp.bfloat16)
        return carry

    lax.fori_loop(0, tile_ref.shape[0] // step, body, 0)


tile_gain = slope / kernel_norm


def matern_tile(rows, cols):
    extent, width = rows.shape[1], cols.shape[1]
    return call(
        tile_body,
        jax.ShapeDtypeStruct((extent, width), jnp.bfloat16),
        (rows, cols),
        scratch=[pltpu.VMEM((extent, 8), jnp.bfloat16), pltpu.VMEM((8, width), jnp.bfloat16)],
    )


def hour_sum(first, own, second):
    hours = own.shape[0]
    turn = 1 - 2 * lax.rem(lax.axis_index("tm"), 2)
    rows = lax.broadcasted_iota(jnp.int32, (hours, 3 * hours), 0)
    cols = lax.broadcasted_iota(jnp.int32, (hours, 3 * hours), 1)
    part = jnp.where(cols >= hours, 1, 0) + jnp.where(cols >= 2 * hours, 1, 0)
    lag = rows - cols + part * hours - (1 - part) * (turn * hours)
    lag = jnp.abs(lag.astype(jnp.float32))
    frac = lag / (hours + 1.0)
    inner = jnp.maximum(1.0 - frac, 0.0)
    squared = inner * inner
    weight = squared * squared * (4.0 * frac + 1.0) / hours
    weight = jnp.where(lag <= hours, weight, 0.0)
    top = weight.astype(jnp.bfloat16)
    rest = (weight - top.astype(jnp.float32)).astype(jnp.bfloat16)
    both = jnp.dot(
        jnp.concatenate([top, rest], axis=0),
        jnp.concatenate([first, own, second], axis=0),
        preferred_element_type=jnp.float32,
    )
    return both[:hours] + both[hours:]


def smooth_body(first_ref, own_ref, second_ref, out_ref):
    out_ref[...] = hour_sum(first_ref[...], own_ref[...], second_ref[...]).astype(out_ref.dtype)


def halo(field):
    count = lax.axis_size("tm")
    halves = []
    for side in (0, 1):
        pairs = [(i, i + 1) for i in range(side, count - 1, 2)]
        if not pairs:
            halves.append(jnp.zeros_like(field))
            continue
        swaps = pairs + [(b, a) for a, b in pairs]
        halves.append(lax.ppermute(field, "tm", swaps))
    return halves


def from_partner(value, offset):
    count = lax.axis_size("stn")
    if count & (count - 1):
        moves = [((i + offset) % count, i) for i in range(count)]
    else:
        moves = [(i ^ offset, i) for i in range(count)]
    return lax.ppermute(value, "stn", moves)


def gathered(value):
    count = lax.axis_size("stn")
    blocks = {0: value}
    for k in range(1, count):
        low = k & -k
        if count & (count - 1) or low == k:
            blocks[k] = from_partner(value, k)
        else:
            moves = [(i ^ low, i) for i in range(count)]
            blocks[k] = lax.ppermute(blocks[k ^ low], "stn", moves)
    return [blocks[k] for k in range(count)]


def product(blocks, tiles):
    total = jnp.dot(blocks[0][...], tiles[0][...], preferred_element_type=jnp.float32)
    for block, tile in zip(blocks[1:], tiles[1:]):
        total += jnp.dot(block[...], tile[...], preferred_element_type=jnp.float32)
    return total


def first_body(count, *refs):
    blocks, tiles = refs[:count], refs[count : 2 * count]
    field, gain, image, masked = refs[2 * count :]
    spread = tile_gain * product(blocks, tiles)
    image[...] = gain[...] * spread + noise_level * field[...]
    masked[...] = (gain[...] * image[...]).astype(masked.dtype)


def part_body(count, *refs):
    refs[-1][...] = product(refs[:count], refs[count : 2 * count])


def more_body(block, tile, before, out):
    out[...] = before[...] + product([block], [tile])


def sum_all(value):
    return jnp.sum(jnp.sum(value, axis=0, keepdims=True), axis=1, keepdims=True)


def second_body(
    block, tile, before, field_ref, image_ref, a0, m0, b0, a1, m1, b1, spread_ref, sums_ref
):
    spread = tile_gain * (before[...] + product([block], [tile]))
    spread_ref[...] = spread.astype(spread_ref.dtype)
    field, image = field_ref[...], image_ref[...]
    norm, along = sum_all(field * field), sum_all(field * image)
    guess = norm / jnp.maximum(jnp.maximum(along, noise_level * norm), 1e-30)
    near = field - guess * image
    values = (
        norm,
        along,
        guess,
        sum_all(near * near),
        sum_all(near * image),
        sum_all(image * image),
        sum_all(hour_sum(a0[...], m0[...], b0[...]) * spread),
        sum_all(hour_sum(a1[...], m1[...], b1[...]) * spread),
    )
    lane = lax.broadcasted_iota(jnp.int32, sums_ref.shape, 1)
    row = jnp.zeros(sums_ref.shape, jnp.float32)
    for index, value in enumerate(values):
        row = jnp.where(lane == index, value, row)
    sums_ref[...] = row


def last_body(sums_ref, field_ref, image_ref, gain_ref, a, own, b, solution_ref, residual_ref):
    sums = sums_ref[...]
    norm, along, guess, near2, near_image, image2, cross0, cross1 = (
        sums[:, k : k + 1] for k in range(8)
    )
    norm_now = sum_all(norm)
    alpha = norm_now / sum_all(along)
    off = alpha - guess
    norm_next = sum_all(near2 - 2.0 * off * near_image + off * off * image2)
    residual_image = sum_all(near_image - off * image2)
    cross = sum_all(cross0) - alpha * sum_all(cross1)
    product_next = residual_image - alpha * (noise_level * residual_image + cross)
    ratio = norm_next / norm_now
    alpha_next = norm_next / (product_next - ratio * norm_next / alpha)
    field, image = field_ref[...], image_ref[...]
    second = gain_ref[...] * hour_sum(a[...], own[...], b[...]) + noise_level * image
    residual = field - alpha * image
    change = (image - alpha * second) + ratio * image
    direction = residual + ratio * field
    solution_ref[...] = alpha * field + alpha_next * direction
    residual_ref[...] = residual - alpha_next * change


def compute(right_side, mask, coords, station_scale):
    count = lax.axis_size("stn")
    everyone = count * lax.axis_size("tm")
    block = jax.ShapeDtypeStruct(right_side.shape, jnp.bfloat16)
    wide = jax.ShapeDtypeStruct(right_side.shape, jnp.float32)

    field, coords, gain, masked = load(right_side, mask, coords, station_scale[None, :])
    before, after = halo(masked)
    tiles = []
    for rows in gathered(coords):
        tiles.append(matern_tile(rows, coords))
    smooth = call(smooth_body, block, (before, masked, after))
    image, image_masked = call(
        functools.partial(first_body, count),
        (wide, block),
        (*gathered(smooth), *tiles, field, gain),
    )
    blocks = gathered(image_masked)
    image_before, image_after = halo(image_masked)
    ready = min(2, count - 1)
    total = call(functools.partial(part_body, ready), wide, (*blocks[:ready], *tiles[:ready]))
    for k in range(ready, count - 1):
        total = call(more_body, wide, (blocks[k], tiles[k], total))
    spread, sums = call(
        second_body,
        (block, jax.ShapeDtypeStruct((everyone, LANES), jnp.float32)),
        (
            *(blocks[-1], tiles[-1], total, field, image),
            *(before, masked, after),
            *(image_before, image_masked, image_after),
        ),
    )
    last_before, last_after = halo(spread)
    sums = lax.all_to_all(sums, ("tm", "stn"), 0, 0, tiled=True)
    return call(
        last_body, (wide, wide), (sums, field, image, gain, last_before, spread, last_after)
    )


def solution(mesh):
    placed = (
        P(("groups", "tm"), "stn"),
        P(("groups", "tm"), "stn"),
        P(None, ("groups", "stn")),
        P(("groups", "stn")),
    )
    return jax.shard_map(
        compute,
        mesh=mesh,
        in_specs=placed,
        out_specs=(P(("groups", "tm"), "stn"), P(("groups", "tm"), "stn")),
        check_vma=False,
    )
```

```python
import functools
import math

import jax
import jax.numpy as jnp
from jax import lax
from jax.experimental import pallas as pl
from jax.experimental.pallas import tpu as pltpu
from jax.sharding import PartitionSpec as P


GRID = 256
kernel_norm = 4.0
noise_level = 0.5
slope = math.sqrt(3.0) * 4.0 / GRID
LANES = 128
MIB = 1024 * 1024
VMEM = pl.BlockSpec(memory_space=pltpu.VMEM)
HBM = pl.BlockSpec(memory_space=pltpu.HBM)


def call(body, out_shape, args, in_specs=None, scratch=()):
    return pl.pallas_call(
        body,
        out_shape=out_shape,
        in_specs=in_specs or [VMEM] * len(args),
        out_specs=jax.tree.map(lambda _: VMEM, out_shape),
        scratch_shapes=list(scratch),
        compiler_params=pltpu.CompilerParams(vmem_limit_bytes=16 * MIB),
    )(*args)


def load_body(field_hbm, mask_hbm, coords_hbm, scale_hbm, field, coords, gain, masked, mask, scale, sems):
    pairs = ((mask_hbm, mask), (scale_hbm, scale.at[0]), (field_hbm, field), (coords_hbm, coords))
    copies = [
        pltpu.make_async_copy(source, target, sems.at[k])
        for k, (source, target) in enumerate(pairs)
    ]
    for copy in copies:
        copy.start()
    for copy in copies:
        copy.wait()
    hours, width = field.shape
    block = hours // mask.shape[0]
    observed = mask[...].astype(jnp.float32)
    observed = jnp.concatenate(
        [jnp.broadcast_to(observed[b : b + 1], (block, width)) for b in range(mask.shape[0])],
        axis=0,
    )
    gain[...] = observed * scale[...]
    masked[...] = (gain[...] * field[...]).astype(masked.dtype)


def load(right_side, mask, coords, scale):
    return call(
        load_body,
        (
            jax.ShapeDtypeStruct(right_side.shape, right_side.dtype),
            jax.ShapeDtypeStruct(coords.shape, coords.dtype),
            jax.ShapeDtypeStruct(right_side.shape, jnp.float32),
            jax.ShapeDtypeStruct(right_side.shape, jnp.bfloat16),
        ),
        [pltpu.with_memory_space_constraint(x, pltpu.HBM) for x in (right_side, mask, coords, scale)],
        in_specs=[HBM] * 4,
        scratch=[
            pltpu.VMEM(mask.shape, mask.dtype),
            pltpu.VMEM((1, *scale.shape), scale.dtype),
            pltpu.SemaphoreType.DMA((4,)),
        ],
    )


def features(coords, rows):
    centred = coords.astype(jnp.float32) - GRID / 2.0
    x, y = centred[0:1], centred[1:2]
    square = x * x + y * y
    high = jnp.floor(square * (1.0 / 256.0)) * 256.0
    low = square - high
    one, zero = jnp.ones_like(x), jnp.zeros_like(x)
    if rows:
        return jnp.concatenate([x, y, high, low, one, one, zero, zero], axis=0)
    return jnp.concatenate([-2.0 * x, -2.0 * y, one, one, high, low, zero, zero], axis=0)


def step_of(extent):
    for step in (896, 512, 256, 128, 64, 32, 16):
        if extent % step == 0:
            return step
    return extent


def tile_body(rows_ref, cols_ref, tile_ref, row_features, col_features):
    row_features[...] = features(rows_ref[...], True).T.astype(jnp.bfloat16)
    col_features[...] = features(cols_ref[...], False).astype(jnp.bfloat16)
    step = step_of(tile_ref.shape[0])

    def body(index, carry):
        at = pl.ds(pl.multiple_of(index * step, step), step)
        square = jnp.dot(
            row_features[at, :], col_features[...], preferred_element_type=jnp.float32
        )
        distance = square * lax.rsqrt(jnp.maximum(square, 1e-20))
        decay = jnp.exp2(distance * (-slope * math.log2(math.e)))
        tile_ref[at, :] = ((1.0 / slope + distance) * decay).astype(jnp.bfloat16)
        return carry

    lax.fori_loop(0, tile_ref.shape[0] // step, body, 0)


tile_gain = slope / kernel_norm


def matern_tile(rows, cols):
    extent, width = rows.shape[1], cols.shape[1]
    return call(
        tile_body,
        jax.ShapeDtypeStruct((extent, width), jnp.bfloat16),
        (rows, cols),
        scratch=[pltpu.VMEM((extent, 8), jnp.bfloat16), pltpu.VMEM((8, width), jnp.bfloat16)],
    )


def hour_sum(first, own, second):
    hours = own.shape[0]
    turn = 1 - 2 * lax.rem(lax.axis_index("tm"), 2)
    rows = lax.broadcasted_iota(jnp.int32, (hours, 3 * hours), 0)
    cols = lax.broadcasted_iota(jnp.int32, (hours, 3 * hours), 1)
    part = jnp.where(cols >= hours, 1, 0) + jnp.where(cols >= 2 * hours, 1, 0)
    lag = rows - cols + part * hours - (1 - part) * (turn * hours)
    lag = jnp.abs(lag.astype(jnp.float32))
    frac = lag / (hours + 1.0)
    inner = jnp.maximum(1.0 - frac, 0.0)
    squared = inner * inner
    weight = squared * squared * (4.0 * frac + 1.0) / hours
    weight = jnp.where(lag <= hours, weight, 0.0)
    top = weight.astype(jnp.bfloat16)
    rest = (weight - top.astype(jnp.float32)).astype(jnp.bfloat16)
    both = jnp.dot(
        jnp.concatenate([top, rest], axis=0),
        jnp.concatenate([first, own, second], axis=0),
        preferred_element_type=jnp.float32,
    )
    return both[:hours] + both[hours:]


def smooth_body(first_ref, own_ref, second_ref, out_ref):
    out_ref[...] = hour_sum(first_ref[...], own_ref[...], second_ref[...]).astype(out_ref.dtype)


def halo(field):
    count = lax.axis_size("tm")
    halves = []
    for side in (0, 1):
        pairs = [(i, i + 1) for i in range(side, count - 1, 2)]
        if not pairs:
            halves.append(jnp.zeros_like(field))
            continue
        swaps = pairs + [(b, a) for a, b in pairs]
        halves.append(lax.ppermute(field, "tm", swaps))
    return halves


def from_partner(value, offset):
    count = lax.axis_size("stn")
    if count & (count - 1):
        moves = [((i + offset) % count, i) for i in range(count)]
    else:
        moves = [(i ^ offset, i) for i in range(count)]
    return lax.ppermute(value, "stn", moves)


def gathered(value):
    count = lax.axis_size("stn")
    blocks = {0: value}
    for k in range(1, count):
        low = k & -k
        if count & (count - 1) or low == k:
            blocks[k] = from_partner(value, k)
        else:
            moves = [(i ^ low, i) for i in range(count)]
            blocks[k] = lax.ppermute(blocks[k ^ low], "stn", moves)
    return [blocks[k] for k in range(count)]


def product(blocks, tiles):
    total = jnp.dot(blocks[0][...], tiles[0][...], preferred_element_type=jnp.float32)
    for block, tile in zip(blocks[1:], tiles[1:]):
        total += jnp.dot(block[...], tile[...], preferred_element_type=jnp.float32)
    return total


def first_body(count, *refs):
    blocks, tiles = refs[:count], refs[count : 2 * count]
    field, gain, image, masked = refs[2 * count :]
    spread = tile_gain * product(blocks, tiles)
    image[...] = gain[...] * spread + noise_level * field[...]
    masked[...] = (gain[...] * image[...]).astype(masked.dtype)


def part_body(count, *refs):
    refs[-1][...] = product(refs[:count], refs[count : 2 * count])


def more_body(block, tile, before, out):
    out[...] = before[...] + product([block], [tile])


def sum_all(value):
    return jnp.sum(jnp.sum(value, axis=0, keepdims=True), axis=1, keepdims=True)


def second_body(block, tile, before, spread):
    spread[...] = (tile_gain * (before[...] + product([block], [tile]))).astype(spread.dtype)


def close_body(field_ref, image_ref, gain_ref, first_ref, own_ref, second_ref, next_ref, sums_ref):
    field, image = field_ref[...], image_ref[...]
    spread = hour_sum(first_ref[...], own_ref[...], second_ref[...])
    following = gain_ref[...] * spread + noise_level * image
    next_ref[...] = following
    norm, along = sum_all(field * field), sum_all(field * image)
    guess = norm / jnp.maximum(jnp.maximum(along, noise_level * norm), 1e-30)
    near = field - guess * image
    near_image = image - guess * following
    values = (
        norm,
        along,
        guess,
        sum_all(near * near),
        sum_all(near * image),
        sum_all(image * image),
        sum_all(near * near_image),
        sum_all(near * following + image * near_image),
        sum_all(image * following),
    )
    lane = lax.broadcasted_iota(jnp.int32, sums_ref.shape, 1)
    row = jnp.zeros(sums_ref.shape, jnp.float32)
    for index, value in enumerate(values):
        row = jnp.where(lane == index, value, row)
    sums_ref[...] = row


def last_body(sums_ref, field_ref, image_ref, next_ref, solution_ref, residual_ref):
    sums = sums_ref[...]
    norm, along, guess, near2, near_image, image2, cross0, cross1, cross2 = (
        sums[:, k : k + 1] for k in range(9)
    )
    norm_now = sum_all(norm)
    alpha = norm_now / sum_all(along)
    off = alpha - guess
    norm_next = sum_all(near2 - 2.0 * off * near_image + off * off * image2)
    product_next = sum_all(cross0 - off * cross1 + off * off * cross2)
    ratio = norm_next / norm_now
    alpha_next = norm_next / (product_next - ratio * norm_next / alpha)
    field, image = field_ref[...], image_ref[...]
    residual = field - alpha * image
    change = (image - alpha * next_ref[...]) + ratio * image
    direction = residual + ratio * field
    solution_ref[...] = alpha * field + alpha_next * direction
    residual_ref[...] = residual - alpha_next * change


def compute(right_side, mask, coords, station_scale):
    count = lax.axis_size("stn")
    everyone = count * lax.axis_size("tm")
    block = jax.ShapeDtypeStruct(right_side.shape, jnp.bfloat16)
    wide = jax.ShapeDtypeStruct(right_side.shape, jnp.float32)

    field, coords, gain, masked = load(right_side, mask, coords, station_scale)
    before, after = halo(masked)
    tiles = []
    for rows in gathered(coords):
        tiles.append(matern_tile(rows, coords))
    smooth = call(smooth_body, block, (before, masked, after))
    image, image_masked = call(
        functools.partial(first_body, count),
        (wide, block),
        (*gathered(smooth), *tiles, field, gain),
    )
    blocks = gathered(image_masked)
    ready = min(2, count - 1)
    total = call(functools.partial(part_body, ready), wide, (*blocks[:ready], *tiles[:ready]))
    for k in range(ready, count - 1):
        total = call(more_body, wide, (blocks[k], tiles[k], total))
    spread = call(second_body, block, (blocks[-1], tiles[-1], total))
    before, after = halo(spread)
    following, sums = call(
        close_body,
        (wide, jax.ShapeDtypeStruct((everyone, LANES), jnp.float32)),
        (field, image, gain, before, spread, after),
    )
    sums = lax.all_to_all(sums, ("tm", "stn"), 0, 0, tiled=True)
    return call(last_body, (wide, wide), (sums, field, image, following))


def solution(mesh):
    placed = (
        P(("groups", "tm"), "stn"),
        P(("groups", "tm"), "stn"),
        P(None, ("groups", "stn")),
        P(("groups", "stn")),
    )
    return jax.shard_map(
        compute,
        mesh=mesh,
        in_specs=placed,
        out_specs=(P(("groups", "tm"), "stn"), P(("groups", "tm"), "stn")),
        check_vma=False,
    )
```

```python
import functools
import math

import jax
import jax.numpy as jnp
from jax import lax
from jax.experimental import pallas as pl
from jax.experimental.pallas import tpu as pltpu
from jax.sharding import PartitionSpec as P


GRID = 256
kernel_norm = 4.0
noise_level = 0.5
slope = math.sqrt(3.0) * 4.0 / GRID
LANES = 128
MIB = 1024 * 1024
VMEM = pl.BlockSpec(memory_space=pltpu.VMEM)
HBM = pl.BlockSpec(memory_space=pltpu.HBM)


def call(body, out_shape, args, in_specs=None, scratch=()):
    return pl.pallas_call(
        body,
        out_shape=out_shape,
        in_specs=in_specs or [VMEM] * len(args),
        out_specs=jax.tree.map(lambda _: VMEM, out_shape),
        scratch_shapes=list(scratch),
        compiler_params=pltpu.CompilerParams(vmem_limit_bytes=16 * MIB),
    )(*args)


def load_body(field_hbm, mask_hbm, coords_hbm, scale_hbm, field, coords, gain, masked, mask, scale, sems):
    pairs = ((mask_hbm, mask), (scale_hbm, scale.at[0]), (field_hbm, field), (coords_hbm, coords))
    copies = [
        pltpu.make_async_copy(source, target, sems.at[k])
        for k, (source, target) in enumerate(pairs)
    ]
    for copy in copies:
        copy.start()
    for copy in copies:
        copy.wait()
    hours, width = field.shape
    block = hours // mask.shape[0]
    observed = mask[...].astype(jnp.float32)
    observed = jnp.concatenate(
        [jnp.broadcast_to(observed[b : b + 1], (block, width)) for b in range(mask.shape[0])],
        axis=0,
    )
    gain[...] = observed * scale[...]
    masked[...] = (gain[...] * field[...]).astype(masked.dtype)


def load(right_side, mask, coords, scale):
    return call(
        load_body,
        (
            jax.ShapeDtypeStruct(right_side.shape, right_side.dtype),
            jax.ShapeDtypeStruct(coords.shape, coords.dtype),
            jax.ShapeDtypeStruct(right_side.shape, jnp.float32),
            jax.ShapeDtypeStruct(right_side.shape, jnp.bfloat16),
        ),
        [pltpu.with_memory_space_constraint(x, pltpu.HBM) for x in (right_side, mask, coords, scale)],
        in_specs=[HBM] * 4,
        scratch=[
            pltpu.VMEM(mask.shape, mask.dtype),
            pltpu.VMEM((1, *scale.shape), scale.dtype),
            pltpu.SemaphoreType.DMA((4,)),
        ],
    )


def features(coords, rows):
    centred = coords.astype(jnp.float32) - GRID / 2.0
    x, y = centred[0:1], centred[1:2]
    square = x * x + y * y
    high = jnp.floor(square * (1.0 / 256.0)) * 256.0
    low = square - high
    one, zero = jnp.ones_like(x), jnp.zeros_like(x)
    if rows:
        return jnp.concatenate([x, y, high, low, one, one, zero, zero], axis=0)
    return jnp.concatenate([-2.0 * x, -2.0 * y, one, one, high, low, zero, zero], axis=0)


def step_of(extent):
    for step in (256, 128, 64, 32, 16):
        if extent % step == 0:
            return step
    return extent


def tile_body(rows_ref, cols_ref, *refs):
    *given, row_features, col_features = refs
    if len(given) == 1:
        (tile_ref,), blocks, befores, total_ref, total = given, (), (), None, None
    else:
        *given, tile_ref, total_ref = given
        pairs = len(given) // 2
        blocks, befores = given[:pairs], given[pairs : 2 * pairs]
        total = given[2 * pairs] if len(given) % 2 else None
    row_features[...] = features(rows_ref[...], True).T.astype(jnp.bfloat16)
    col_features[...] = features(cols_ref[...], False).astype(jnp.bfloat16)
    extent = tile_ref.shape[0]
    step = step_of(extent)
    for start in range(0, extent, step):
        at = pl.ds(start, step)
        square = jnp.dot(
            row_features[at, :], col_features[...], preferred_element_type=jnp.float32
        )
        distance = square * lax.rsqrt(jnp.maximum(square, 1e-20))
        decay = jnp.exp2(distance * (-slope * math.log2(math.e)))
        tile_ref[at, :] = ((1.0 / slope + distance) * decay).astype(jnp.bfloat16)
        for index, (block, before) in enumerate(zip(blocks, befores)):
            part = jnp.dot(block[:, at], before[at, :], preferred_element_type=jnp.float32)
            if index or start:
                part += total_ref[...]
            elif total is not None:
                part += total[...]
            total_ref[...] = part


tile_gain = slope / kernel_norm


def matern_tile(rows, cols, blocks=(), tiles=(), total=None):
    extent, width = rows.shape[1], cols.shape[1]
    tile = jax.ShapeDtypeStruct((extent, width), jnp.bfloat16)
    out = tile
    if blocks:
        out = (tile, jax.ShapeDtypeStruct((blocks[0].shape[0], width), jnp.float32))
    return call(
        tile_body,
        out,
        (rows, cols, *blocks, *tiles, *(() if total is None else (total,))),
        scratch=[pltpu.VMEM((extent, 8), jnp.bfloat16), pltpu.VMEM((8, width), jnp.bfloat16)],
    )


def hour_sum(first, own, second):
    hours = own.shape[0]
    turn = 1 - 2 * lax.rem(lax.axis_index("tm"), 2)
    rows = lax.broadcasted_iota(jnp.int32, (hours, 3 * hours), 0)
    cols = lax.broadcasted_iota(jnp.int32, (hours, 3 * hours), 1)
    part = jnp.where(cols >= hours, 1, 0) + jnp.where(cols >= 2 * hours, 1, 0)
    lag = rows - cols + part * hours - (1 - part) * (turn * hours)
    lag = jnp.abs(lag.astype(jnp.float32))
    frac = lag / (hours + 1.0)
    inner = jnp.maximum(1.0 - frac, 0.0)
    squared = inner * inner
    weight = squared * squared * (4.0 * frac + 1.0) / hours
    weight = jnp.where(lag <= hours, weight, 0.0)
    top = weight.astype(jnp.bfloat16)
    rest = (weight - top.astype(jnp.float32)).astype(jnp.bfloat16)
    both = jnp.dot(
        jnp.concatenate([top, rest], axis=0),
        jnp.concatenate([first, own, second], axis=0),
        preferred_element_type=jnp.float32,
    )
    return both[:hours] + both[hours:]


def smooth_body(first_ref, own_ref, second_ref, out_ref):
    out_ref[...] = hour_sum(first_ref[...], own_ref[...], second_ref[...]).astype(out_ref.dtype)


def halo(field):
    count = lax.axis_size("tm")
    halves = []
    for side in (0, 1):
        pairs = [(i, i + 1) for i in range(side, count - 1, 2)]
        if not pairs:
            halves.append(jnp.zeros_like(field))
            continue
        swaps = pairs + [(b, a) for a, b in pairs]
        halves.append(lax.ppermute(field, "tm", swaps))
    return halves


def from_partner(value, offset):
    count = lax.axis_size("stn")
    if count & (count - 1):
        moves = [((i + offset) % count, i) for i in range(count)]
    else:
        moves = [(i ^ offset, i) for i in range(count)]
    return lax.ppermute(value, "stn", moves)


def gathered(value):
    count = lax.axis_size("stn")
    blocks = {0: value}
    for k in range(1, count):
        low = k & -k
        if count & (count - 1) or low == k:
            blocks[k] = from_partner(value, k)
        else:
            moves = [(i ^ low, i) for i in range(count)]
            blocks[k] = lax.ppermute(blocks[k ^ low], "stn", moves)
    return [blocks[k] for k in range(count)]


def product(blocks, tiles):
    total = jnp.dot(blocks[0][...], tiles[0][...], preferred_element_type=jnp.float32)
    for block, tile in zip(blocks[1:], tiles[1:]):
        total += jnp.dot(block[...], tile[...], preferred_element_type=jnp.float32)
    return total


def first_body(count, *refs):
    blocks, tiles = refs[:count], refs[count : 2 * count]
    total, field, gain, image, masked = refs[2 * count :]
    spread = tile_gain * (total[...] + product(blocks, tiles))
    image[...] = gain[...] * spread + noise_level * field[...]
    masked[...] = (gain[...] * image[...]).astype(masked.dtype)


def part_body(count, *refs):
    refs[-1][...] = product(refs[:count], refs[count : 2 * count])


def more_body(block, tile, before, out):
    out[...] = before[...] + product([block], [tile])


def sum_all(value):
    return jnp.sum(jnp.sum(value, axis=0, keepdims=True), axis=1, keepdims=True)


def second_body(
    block, tile, before, field_ref, image_ref, a0, m0, b0, a1, m1, b1, spread_ref, sums_ref
):
    spread = tile_gain * (before[...] + product([block], [tile]))
    spread_ref[...] = spread.astype(spread_ref.dtype)
    field, image = field_ref[...], image_ref[...]
    norm, along = sum_all(field * field), sum_all(field * image)
    guess = norm / jnp.maximum(jnp.maximum(along, noise_level * norm), 1e-30)
    near = field - guess * image
    values = (
        norm,
        along,
        guess,
        sum_all(near * near),
        sum_all(near * image),
        sum_all(image * image),
        sum_all(hour_sum(a0[...], m0[...], b0[...]) * spread),
        sum_all(hour_sum(a1[...], m1[...], b1[...]) * spread),
    )
    lane = lax.broadcasted_iota(jnp.int32, sums_ref.shape, 1)
    row = jnp.zeros(sums_ref.shape, jnp.float32)
    for index, value in enumerate(values):
        row = jnp.where(lane == index, value, row)
    sums_ref[...] = row


def last_body(sums_ref, field_ref, image_ref, gain_ref, a, own, b, solution_ref, residual_ref):
    sums = sums_ref[...]
    norm, along, guess, near2, near_image, image2, cross0, cross1 = (
        sums[:, k : k + 1] for k in range(8)
    )
    norm_now = sum_all(norm)
    alpha = norm_now / sum_all(along)
    off = alpha - guess
    norm_next = sum_all(near2 - 2.0 * off * near_image + off * off * image2)
    residual_image = sum_all(near_image - off * image2)
    cross = sum_all(cross0) - alpha * sum_all(cross1)
    product_next = residual_image - alpha * (noise_level * residual_image + cross)
    ratio = norm_next / norm_now
    alpha_next = norm_next / (product_next - ratio * norm_next / alpha)
    field, image = field_ref[...], image_ref[...]
    second = gain_ref[...] * hour_sum(a[...], own[...], b[...]) + noise_level * image
    residual = field - alpha * image
    change = (image - alpha * second) + ratio * image
    direction = residual + ratio * field
    solution_ref[...] = alpha * field + alpha_next * direction
    residual_ref[...] = residual - alpha_next * change


def compute(right_side, mask, coords, station_scale):
    count = lax.axis_size("stn")
    everyone = count * lax.axis_size("tm")
    block = jax.ShapeDtypeStruct(right_side.shape, jnp.bfloat16)
    wide = jax.ShapeDtypeStruct(right_side.shape, jnp.float32)

    field, coords, gain, masked = load(right_side, mask, coords, station_scale)
    before, after = halo(masked)
    smooth = call(smooth_body, block, (before, masked, after))
    rows, ring = gathered(coords), gathered(smooth)
    tiles, total, used = [], None, 0
    for k in range(count):
        ready = k
        if ready > used:
            tile, total = matern_tile(rows[k], coords, ring[used:ready], tiles[used:ready], total)
        else:
            tile = matern_tile(rows[k], coords)
        used = max(used, ready)
        tiles.append(tile)
    if total is None:
        total = jnp.zeros(right_side.shape, jnp.float32)
    image, image_masked = call(
        functools.partial(first_body, count - used),
        (wide, block),
        (*ring[used:], *tiles[used:], total, field, gain),
    )
    blocks = gathered(image_masked)
    image_before, image_after = halo(image_masked)
    ready = min(2, count - 1)
    total = call(functools.partial(part_body, ready), wide, (*blocks[:ready], *tiles[:ready]))
    for k in range(ready, count - 1):
        total = call(more_body, wide, (blocks[k], tiles[k], total))
    spread, sums = call(
        second_body,
        (block, jax.ShapeDtypeStruct((everyone, LANES), jnp.float32)),
        (
            *(blocks[-1], tiles[-1], total, field, image),
            *(before, masked, after),
            *(image_before, image_masked, image_after),
        ),
    )
    last_before, last_after = halo(spread)
    sums = lax.all_to_all(sums, ("tm", "stn"), 0, 0, tiled=True)
    return call(
        last_body, (wide, wide), (sums, field, image, gain, last_before, spread, last_after)
    )


def solution(mesh):
    placed = (
        P(("groups", "tm"), "stn"),
        P(("groups", "tm"), "stn"),
        P(None, ("groups", "stn")),
        P(("groups", "stn")),
    )
    return jax.shard_map(
        compute,
        mesh=mesh,
        in_specs=placed,
        out_specs=(P(("groups", "tm"), "stn"), P(("groups", "tm"), "stn")),
        check_vma=False,
    )
```
